32 devices in a mesh: dp: 4 (over y, x), vocab: 8 (over z, core).
Axes of the slice: x: 2, y: 2, z: 4, core: 2. Of those that a mesh axis runs over, the one named last changes fastest.
Arguments:
- prefill_hidden: bfloat16 [128, 7168], P(('dp', 'vocab')), may hold values from -60 to 60
- decode_hidden: bfloat16 [32, 7168], P(('dp', 'vocab')), may hold values from -60 to 60
- lm_head: bfloat16 [7168, 16160], P('dp', 'vocab'), as said below
- prefill_targets: int32 [128], P(('dp', 'vocab')), may hold values from 0 to 16159
- decode_targets: int32 [32], P(('dp', 'vocab')), may hold values from 0 to 16159
- decode_live: int32 [4], P('dp'), may hold values from 1 to 8
Outputs:
- prefill_logprob: float32 [128], P(('dp', 'vocab'))
- decode_logprob: float32 [32], P(('dp', 'vocab'))
The draws below stay inside these ranges and needn't reach their ends.
Inputs may be any that keep to these rules, and one draw needn't show every extreme that they name: `lm_head`: entries of order one over the square root of 7168.
All inputs are finite; a program needn't handle non-finite values.
Results may differ from the reference program's by a relative error of at most 0.0003.
Values may be sent and summed in bfloat16 or wider, within the bound.
No kernel may reach another device: no remote copies, remote signals or barrier semaphores. Data moves between devices by JAX's collectives and lax.ppermute only.
A program may use at most 128 MiB of HBM per device.

```python
import jax
import jax.numpy as jnp
from jax import lax

D = 7168
VOC_DEV = 2020
VOCAB = 16160
PRE_ROWS = 128
DEC_ROWS = 32
DEC_GROUP = 8
N_DP = 4
N_VOCAB = 8


def head_matrix(key):
    base_key = jax.random.fold_in(key, 7001)
    values = jnp.clip(jax.random.normal(jax.random.fold_in(base_key, 1), (D, VOCAB), jnp.float32), -4.0, 4.0) / jnp.sqrt(jnp.float32(D))
    return values


def draw_lm_head(key, part):
    return head_matrix(key).astype(jnp.bfloat16)


def hidden_rows(key, salt_value, row_count):
    row_key = jax.random.fold_in(key, salt_value)
    values = jnp.clip(3.0 * jax.random.normal(jax.random.fold_in(row_key, 6), (row_count, D), jnp.float32), -18.0, 18.0)
    return values.astype(jnp.bfloat16)


def draw_prefill_hidden(key, part):
    return hidden_rows(key, 11, PRE_ROWS)


def draw_decode_hidden(key, part):
    return hidden_rows(key, 13, DEC_ROWS)


def set_ends(drawn, rng, smallest, largest):
    shape = drawn.shape
    spot = [jax.random.randint(jax.random.fold_in(rng, axis), (), 0, shape[axis]) for axis in range(len(shape))]
    drawn = drawn.at[tuple(spot)].set(smallest)
    longest = shape.index(max(shape))
    spot[longest] = (spot[longest] + 1) % shape[longest]
    return drawn.at[tuple(spot)].set(largest)


def setup_inputs(seed: int = 0) -> dict:
    arg_keys = jax.random.split(jax.random.key(seed), 7)
    prefill_hidden = draw_prefill_hidden(jax.random.fold_in(arg_keys[6], 71), 0)
    decode_hidden = draw_decode_hidden(jax.random.fold_in(arg_keys[6], 71), 0)
    lm_head = draw_lm_head(jax.random.fold_in(arg_keys[6], 71), 0)
    prefill_targets = set_ends(jax.random.randint(arg_keys[3], (PRE_ROWS,), 0, VOCAB), jax.random.fold_in(arg_keys[3], 1), 0, VOCAB - 1).astype(jnp.int32)
    decode_targets = set_ends(jax.random.randint(arg_keys[4], (DEC_ROWS,), 0, VOCAB), jax.random.fold_in(arg_keys[4], 1), 0, VOCAB - 1).astype(jnp.int32)
    decode_live = set_ends(jax.random.randint(arg_keys[5], (N_DP,), 1, DEC_GROUP + 1), jax.random.fold_in(arg_keys[5], 1), 1, DEC_GROUP).astype(jnp.int32)
    return {"prefill_hidden": prefill_hidden, "decode_hidden": decode_hidden, "lm_head": lm_head, "prefill_targets": prefill_targets, "decode_targets": decode_targets, "decode_live": decode_live}


def row_logprob(hidden, targets, lm_head):
    row_count = hidden.shape[0]
    columns = jnp.arange(VOC_DEV, dtype=jnp.int32)

    def advance(running, block_index):
        row_top, totals, picked = running
        offset = (block_index * VOC_DEV).astype(jnp.int32)
        head_block = lax.dynamic_slice_in_dim(lm_head, offset, VOC_DEV, 1)
        logits = jnp.dot(hidden, head_block, preferred_element_type=jnp.float32)
        new_top = jnp.maximum(row_top, jnp.max(logits, axis=1))
        totals = totals * jnp.exp(row_top - new_top) + jnp.sum(jnp.exp(logits - new_top[:, None]), axis=1)
        target_hit = (targets - offset)[:, None] == columns[None, :]
        picked = picked + jnp.sum(jnp.where(target_hit, logits, jnp.float32(0.0)), axis=1)
        return (new_top, totals, picked), None

    initial = (jnp.full((row_count,), -jnp.inf, jnp.float32), jnp.zeros((row_count,), jnp.float32), jnp.zeros((row_count,), jnp.float32))
    (row_top, totals, picked), _ = lax.scan(advance, initial, jnp.arange(N_VOCAB, dtype=jnp.int32))
    return picked - (row_top + jnp.log(totals))


def reference(prefill_hidden, decode_hidden, lm_head, prefill_targets, decode_targets, decode_live):
    prefill_logprob = row_logprob(prefill_hidden, prefill_targets, lm_head)
    decode_values = row_logprob(decode_hidden, decode_targets, lm_head)
    positions = jnp.arange(DEC_ROWS, dtype=jnp.int32)
    group_live = decode_live[positions // DEC_GROUP]
    decode_logprob = jnp.where(positions % DEC_GROUP < group_live, decode_values, jnp.float32(0.0))
    return prefill_logprob, decode_logprob
```

```python
import functools

import jax
import jax.numpy as jnp
from jax import lax
from jax.experimental import pallas as pl
from jax.experimental.pallas import tpu as pltpu
from jax.sharding import PartitionSpec as P


BASE = 128
WIRE = jnp.int16
MOST = 32000.0
TINY = 1e-30
STEP = 512
BLOCK = 16
VMEM = pl.BlockSpec(memory_space=pltpu.VMEM)
SMEM = pl.BlockSpec(memory_space=pltpu.SMEM)


def call(kernel, outs, *args, specs, out_specs=None, scratch=(), limit=16 << 20, cost=None):
    return pl.pallas_call(
        kernel,
        out_shape=outs,
        in_specs=specs,
        out_specs=out_specs if out_specs is not None else jax.tree.map(lambda _: VMEM, outs),
        scratch_shapes=scratch,
        compiler_params=pltpu.CompilerParams(vmem_limit_bytes=limit),
        cost_estimate=cost,
    )(*args)


def shape(dims, dtype):
    return jax.ShapeDtypeStruct(dims, dtype)


def split_kernel(n_dp, pre_ref, dec_ref, *out_refs):
    me = lax.axis_index("dp")
    pre, quarter = pre_ref.shape[0], pre_ref.shape[1] // n_dp
    dec = dec_ref.shape[0]
    for k in range(1, n_dp):
        start = pl.multiple_of((me ^ k) * quarter, 128)
        out_refs[k - 1][0:pre, :] = pre_ref[:, pl.ds(start, quarter)]
        out_refs[k - 1][pre : pre + dec, :] = dec_ref[:, pl.ds(start, quarter)]


def dense_kernel(n_dp, pre_ref, dec_ref, r1, r2, r3, pt_ref, dt_ref, out_ref):
    me = lax.axis_index("dp")
    pre, quarter = pre_ref.shape[0], pre_ref.shape[1] // n_dp
    half = quarter // 2
    start = pl.multiple_of(me * quarter, 128)
    pres = [pre_ref[:, pl.ds(start, quarter)]] + [r[0:pre, :] for r in (r1, r2, r3)]
    decs = [dec_ref[:, pl.ds(start, quarter)]] + [r[pre : pre + 1, :] for r in (r1, r2, r3)]
    f32 = jnp.float32
    for pair in range(2):
        both = jnp.concatenate([pres[2 * pair].astype(f32), pres[2 * pair + 1].astype(f32)], axis=0)
        out_ref[:, pair * quarter : (pair + 1) * quarter] = both.astype(jnp.bfloat16)
    wide = [d.astype(f32) for d in decs]
    rows = [d[:, :half] for d in wide] + [d[:, half:] for d in wide]
    index = lax.broadcasted_iota(jnp.int32, (8, half), 0)
    total = jnp.zeros((8, half), f32)
    for i, row in enumerate(rows):
        total = jnp.where(index == i, jnp.broadcast_to(row, (8, half)), total)
    out_ref[:, 2 * quarter : 2 * quarter + half] = total.astype(jnp.bfloat16)
    row = lax.broadcasted_iota(jnp.int32, (8, BASE), 0)
    lane = lax.broadcasted_iota(jnp.int32, (8, BASE), 1)
    ids = jnp.zeros((8, BASE), jnp.int32)
    for i in range(pre):
        ids = jnp.where(row == i, pt_ref[i], ids)
    ids = jnp.where(row == pre, dt_ref[0], ids)
    digit = jnp.where(lane == 0, ids % BASE, jnp.where(lane == 1, (ids // BASE) % BASE, ids // (BASE * BASE)))
    out_ref[:, 2 * quarter + half :] = digit.astype(f32).astype(jnp.bfloat16)


def matmul_kernel(n_dp, n_kv, pre, step, head_ref, *refs):
    bufs = refs[:n_kv]
    outs = refs[n_kv : n_kv + n_dp]
    tgt_ref = refs[n_kv + n_dp]
    x_ref, last_ref = refs[n_kv + n_dp + 1 :]
    voc, quarter = head_ref.shape
    half = quarter // 2
    f32 = jnp.float32
    pre_rows = pre * n_kv
    tgt_ref[...] = jnp.zeros_like(tgt_ref)
    for kv, buf in enumerate(bufs):
        for pair in range(2):
            block = buf[:, pair * quarter : (pair + 1) * quarter].astype(f32)
            for j in range(2):
                k = 2 * pair + j
                x_ref[k * pre_rows + pre * kv : k * pre_rows + pre * (kv + 1), :] = block[4 * j : 4 * j + 4]
        block = buf[:, 2 * quarter : 2 * quarter + half].astype(f32)
        for k in range(n_dp):
            row = n_dp * pre_rows + n_kv * k + kv
            x_ref[row : row + 1, :half] = block[k : k + 1]
            x_ref[row : row + 1, half:] = block[n_dp + k : n_dp + k + 1]
        digits = buf[:, 2 * quarter + half :].astype(f32)
        tgt_ref[pre * kv : pre * (kv + 1), :] = digits[:pre]
        tgt_ref[pre_rows + kv : pre_rows + kv + 1, :] = digits[pre : pre + 1]
    x = x_ref[...].astype(jnp.bfloat16)
    wide = -(-voc // 128) * 128
    powers = []
    for start in range(0, wide, step):
        stop = min(start + step, voc)
        y = lax.dot_general(
            x, head_ref[start:stop, :], (((1,), (1,)), ((), ())), preferred_element_type=f32
        )
        most = jnp.maximum(jnp.max(jnp.abs(y), axis=1, keepdims=True), TINY)
        power = jnp.ceil(jnp.log2(most * (1.0 / MOST)))
        powers.append(power)
        code = jnp.round(y * jnp.exp2(-power))
        if start + step >= wide:
            last_ref[:, : stop - start] = code
            for i, p in enumerate(powers):
                last_ref[:, stop - start + i : stop - start + i + 1] = p
            stop = wide
            code = last_ref[:, : stop - start]
        tail = n_dp * pre_rows
        outs[0][:pre_rows, start : start + y.shape[1]] = y[:pre_rows]
        outs[0][pre_rows:, start : start + y.shape[1]] = y[tail : tail + n_kv]
        code = code.astype(jnp.int32)
        for k in range(1, n_dp):
            piece = [code[k * pre_rows : (k + 1) * pre_rows], code[tail + n_kv * k : tail + n_kv * (k + 1)]]
            outs[k][:, start:stop] = jnp.concatenate(piece, axis=0).astype(WIRE)


def stats_kernel(n_kv, pre, own_ref, p1, p2, p3, tgt_ref, out_ref, tile_ref):
    f32 = jnp.float32
    voc = own_ref.shape[1]
    tiles = []
    for start in range(0, p1.shape[1], STEP):
        stop = min(start + STEP, voc)
        tile = own_ref[:, start:stop]
        for p in (p1, p2, p3):
            lane = voc + start // STEP
            power = p[:, lane : lane + 1].astype(f32)
            tile = tile + p[:, start:stop].astype(f32) * jnp.exp2(power)
        tiles.append(tile)
    s = jnp.concatenate(tiles, axis=1)
    digits = tgt_ref[...]
    ids = digits[:, 0:1] + BASE * digits[:, 1:2] + (BASE * BASE) * digits[:, 2:3]
    local = ids.astype(jnp.int32) - lax.axis_index("vocab") * voc
    columns = lax.broadcasted_iota(jnp.int32, s.shape, 1)
    top = jnp.max(s, axis=1, keepdims=True)
    total = jnp.sum(jnp.exp(s - top), axis=1, keepdims=True)
    picked = jnp.sum(jnp.where(columns == local, s, 0.0), axis=1, keepdims=True)
    lane = lax.broadcasted_iota(jnp.int32, (s.shape[0], 128), 1)
    st = jnp.where(lane == 0, top, jnp.where(lane == 1, total, picked))
    tile_ref[...] = jnp.zeros_like(tile_ref)
    for kv in range(n_kv):
        tile_ref[BLOCK * kv : BLOCK * kv + pre, :] = st[pre * kv : pre * (kv + 1)]
        tile_ref[BLOCK * kv + pre : BLOCK * kv + pre + 1, :] = st[pre * n_kv + kv : pre * n_kv + kv + 1]
    out_ref[...] = jnp.transpose(tile_ref[...])[:8, :]


def merge(a, b):
    top = jnp.maximum(a[0:1], b[0:1])
    total = a[1:2] * jnp.exp(a[0:1] - top) + b[1:2] * jnp.exp(b[0:1] - top)
    return jnp.concatenate([top, total, a[2:3] + b[2:3]], axis=0)


def pair_kernel(mine_ref, other_ref, out_ref):
    other = pltpu.roll(other_ref[...], 64, 1)
    out_ref[0:3, :] = merge(mine_ref[...], other)
    out_ref[3:8, :] = jnp.zeros((5, 128), jnp.float32)


def final_kernel(pre, dec, mine_ref, r1, r2, r3, live_ref, pre_ref, dec_ref):
    total = mine_ref[...]
    for k, r in enumerate((r1, r2, r3), start=1):
        total = merge(total, pltpu.roll(r[...], 128 - BLOCK * k, 1))
    value = total[2:3] - (total[0:1] + jnp.log(total[1:2]))
    position = lax.axis_index("vocab") * dec
    pre_ref[...] = value[0, :pre]
    dec_ref[...] = jnp.where(position < live_ref[0], value[0, pre : pre + dec], 0.0)


def fast_body(n_dp, n_vocab, pre_hidden, dec_hidden, lm_head, pre_targets, dec_targets, dec_live):
    pre, dec = pre_hidden.shape[0], dec_hidden.shape[0]
    quarter, voc = lm_head.shape
    n_z = n_vocab // 2
    bf16, f32 = jnp.bfloat16, jnp.float32

    def swap(x, axis, k):
        return lax.ppermute(x, axis, [(i, i ^ k) for i in range(n_dp if axis == "dp" else n_vocab)])

    sends = call(
        functools.partial(split_kernel, n_dp),
        [shape((8, quarter), bf16)] * (n_dp - 1),
        pre_hidden,
        dec_hidden,
        specs=[VMEM, VMEM],
    )
    got = [swap(s, "dp", k) for k, s in enumerate(sends, start=1)]
    width = 2 * quarter + quarter // 2 + BASE
    mine = call(
        functools.partial(dense_kernel, n_dp),
        shape((8, width), bf16),
        pre_hidden,
        dec_hidden,
        *got,
        pre_targets,
        dec_targets,
        specs=[VMEM] * 5 + [SMEM] * 2,
    )
    chips = [mine] + [swap(mine, "vocab", 2 * k) for k in range(1, n_z)]
    bufs = chips + [swap(b, "vocab", 1) for b in chips]

    group = n_vocab * (pre + dec)
    rows = n_dp * group
    wide = -(-voc // 128) * 128
    outs = [shape((group, voc), f32)] + [shape((group, wide), WIRE)] * (n_dp - 1)
    *parts, tgt = call(
        functools.partial(matmul_kernel, n_dp, n_vocab, pre, STEP),
        outs + [shape((group, BASE), f32)],
        lm_head.T,
        *bufs,
        specs=[VMEM] * (1 + n_vocab),
        scratch=[pltpu.VMEM((rows, quarter), f32), pltpu.VMEM((rows, STEP), f32)],
        limit=32 << 20,
        cost=pl.CostEstimate(flops=2 * rows * quarter * voc, bytes_accessed=2 * quarter * voc, transcendentals=0),
    )
    arrived = [swap(p, "dp", k) for k, p in enumerate(parts[1:], start=1)]
    stats = call(
        functools.partial(stats_kernel, n_vocab, pre),
        shape((8, 128), f32),
        parts[0],
        *arrived,
        tgt,
        specs=[VMEM] * 5,
        scratch=[pltpu.VMEM((128, 128), f32)],
    )
    both = call(pair_kernel, shape((8, 128), f32), stats, swap(stats, "vocab", 1), specs=[VMEM] * 2)
    others = [swap(both, "vocab", 2 * k) for k in range(1, n_z)]
    return tuple(
        call(
            functools.partial(final_kernel, pre, dec),
            [shape((pre,), f32), shape((dec,), f32)],
            both,
            *others,
            dec_live,
            specs=[VMEM] * n_z + [SMEM],
        )
    )


def plain_body(pre_hidden, dec_hidden, lm_head, pre_targets, dec_targets, dec_live):
    pre, dec = pre_hidden.shape[0], dec_hidden.shape[0]
    own = pre + dec
    voc = lm_head.shape[1]
    hidden = jnp.concatenate([pre_hidden, dec_hidden], axis=0)
    targets = jnp.concatenate([pre_targets, dec_targets], axis=0)
    me = lax.axis_index("vocab")
    group_hidden = lax.all_gather(hidden, "vocab", axis=0, tiled=True)
    group_targets = lax.all_gather(targets, "vocab", axis=0, tiled=True)
    every = lax.all_to_all(group_hidden, "dp", split_axis=1, concat_axis=0, tiled=True)
    partial = jnp.dot(every, lm_head, preferred_element_type=jnp.float32)
    logits = lax.psum_scatter(partial, "dp", scatter_dimension=0, tiled=True)
    hit = (group_targets - me * voc)[:, None] == jnp.arange(voc, dtype=jnp.int32)[None, :]
    picked = jnp.sum(jnp.where(hit, logits, 0.0), axis=1)
    top = lax.pmax(jnp.max(logits, axis=1), "vocab")
    total = jnp.sum(jnp.exp(logits - top[:, None]), axis=1)
    total, picked = lax.psum((total, picked), "vocab")
    values = lax.dynamic_slice_in_dim(picked - (top + jnp.log(total)), me * own, own, 0)
    positions = me * dec + jnp.arange(dec, dtype=jnp.int32)
    return values[:pre], jnp.where(positions < dec_live[0], values[pre:], 0.0)


def solution(mesh):
    n_dp, n_vocab = mesh.shape["dp"], mesh.shape["vocab"]

    def body(pre_hidden, dec_hidden, *rest):
        small = n_dp == 4 and n_vocab == 8 and pre_hidden.shape[0] == 4 and dec_hidden.shape[0] == 1
        run = functools.partial(fast_body, n_dp, n_vocab) if small else plain_body
        return run(pre_hidden, dec_hidden, *rest)

    rows = P(("dp", "vocab"))
    in_specs = (P(("dp", "vocab"), None), P(("dp", "vocab"), None), P("dp", "vocab"), rows, rows, P("dp"))
    return jax.shard_map(body, mesh=mesh, in_specs=in_specs, out_specs=(rows, rows), check_vma=False)
```

```python
import functools

import jax
import jax.numpy as jnp
from jax import lax
from jax.experimental import pallas as pl
from jax.experimental.pallas import tpu as pltpu
from jax.sharding import PartitionSpec as P


BASE = 128
WIRE = jnp.int16
MOST = 32000.0
TINY = 1e-30
CHUNKS = 1
TILES = 4
BLOCK = 16
VMEM = pl.BlockSpec(memory_space=pltpu.VMEM)
SMEM = pl.BlockSpec(memory_space=pltpu.SMEM)
HBM = pl.BlockSpec(memory_space=pltpu.HBM)
F32, BF16 = jnp.float32, jnp.bfloat16


def call(kernel, outs, *args, specs, scratch=(), limit=8 << 20, flops=0, moved=0):
    return pl.pallas_call(
        kernel,
        out_shape=outs,
        in_specs=specs,
        out_specs=jax.tree.map(lambda _: VMEM, outs),
        scratch_shapes=scratch,
        compiler_params=pltpu.CompilerParams(vmem_limit_bytes=limit),
        cost_estimate=pl.CostEstimate(flops=flops, bytes_accessed=moved, transcendentals=0),
    )(*args)


def far(x):
    return pltpu.with_memory_space_constraint(x, pltpu.HBM)


def shape(dims, dtype):
    return jax.ShapeDtypeStruct(dims, dtype)


def sublane(block):
    return lax.broadcasted_iota(jnp.int32, block, 0)


def spread(rows, block):
    out = jnp.zeros(block, F32)
    for i, row in rows.items():
        out = jnp.where(sublane(block) == i, jnp.broadcast_to(row, block), out)
    return out


def part(pre_ref, dec_ref, index):
    quarter = pre_ref.shape[1] // 4
    start = pl.multiple_of(index * quarter, 128)
    return pre_ref[:, pl.ds(start, quarter)].astype(F32), dec_ref[:, pl.ds(start, quarter)].astype(F32)


def load_kernel(pre_hbm, dec_hbm, pre_ref, dec_ref, *refs):
    outs, sems = refs[:-1], refs[-1]
    copies = [
        pltpu.make_async_copy(pre_hbm, pre_ref, sems.at[0]),
        pltpu.make_async_copy(dec_hbm, dec_ref, sems.at[1]),
    ]
    for c in copies:
        c.start()
    for c in copies:
        c.wait()
    me = lax.axis_index("dp")
    for k, out_ref in enumerate(outs, start=1):
        pre, dec = part(pre_ref, dec_ref, me ^ k)
        half = pre.shape[1] // 2
        out_ref[:, :half] = jnp.concatenate([pre[:, :half], pre[:, half:]], axis=0).astype(BF16)
        out_ref[:, half:] = fold(dec).astype(BF16)


def fold(row):
    each = -(-row.shape[1] // 1024) * 128
    rows = {}
    for i in range(8):
        low, high = min(i * each, row.shape[1]), min((i + 1) * each, row.shape[1])
        if high > low:
            rows[i] = row[:, low:high]
            if high - low < each:
                rows[i] = jnp.concatenate([rows[i], jnp.zeros((1, each - high + low), row.dtype)], axis=1)
    return spread(rows, (8, each))


def unfold(block, width):
    return jnp.concatenate([block[i : i + 1] for i in range(8)], axis=1)[:, :width]


def ids_kernel(pre, pt_ref, dt_ref, live_ref, ids_ref, live_out):
    lane = lax.broadcasted_iota(jnp.int32, (8, BASE), 1)
    ids = jnp.zeros((8, BASE), jnp.int32)
    for i in range(pre):
        ids = jnp.where(sublane(ids.shape) == i, pt_ref[i], ids)
    ids = jnp.where(sublane(ids.shape) == pre, dt_ref[0], ids)
    low, mid, high = ids & (BASE - 1), (ids >> 7) & (BASE - 1), ids >> 14
    ids_ref[...] = jnp.where(lane == 0, low, jnp.where(lane == 1, mid, high)).astype(F32).astype(BF16)
    live_out[...] = jnp.broadcast_to(live_ref[0], live_out.shape)


def dense_kernel(pre_ref, dec_ref, r1, r2, r3, ids_ref, out_ref):
    sets = [part(pre_ref, dec_ref, lax.axis_index("dp"))]
    quarter = sets[0][0].shape[1]
    half = quarter // 2
    for r in (r1, r2, r3):
        pre = r[:, :half].astype(F32)
        sets.append((jnp.concatenate([pre[:4], pre[4:]], axis=1), unfold(r[:, half:].astype(F32), quarter)))
    for pair in range(2):
        both = jnp.concatenate([sets[2 * pair][0], sets[2 * pair + 1][0]], axis=0)
        out_ref[:, pair * quarter : (pair + 1) * quarter] = both.astype(BF16)
    rows = {k + 4 * h: s[1][:, h * half : (h + 1) * half] for k, s in enumerate(sets) for h in range(2)}
    out_ref[:, 2 * quarter : 2 * quarter + half] = spread(rows, (8, half)).astype(BF16)
    out_ref[:, 2 * quarter + half :] = ids_ref[...]


def fetch_kernel(parts, head_hbm, out_ref, sems):
    rows = out_ref.shape[0]
    step = -(-(rows // parts) // 8) * 8
    copies = []
    for i in range(parts):
        block = pl.ds(i * step, min((i + 1) * step, rows) - i * step)
        copies.append(pltpu.make_async_copy(head_hbm.at[block], out_ref.at[block], sems.at[i]))
    for c in copies:
        c.start()
    for c in copies:
        c.wait()


def matmul_kernel(n_dp, pre, voc, *refs):
    head_ref, refs = refs[0], refs[1:]
    n_kv = len(refs) - n_dp - 3
    bufs, refs = refs[:n_kv], refs[n_kv:]
    own_ref, outs, tgt_ref, x_ref, last_ref = refs[0], refs[1:n_dp], refs[n_dp], refs[n_dp + 1], refs[n_dp + 2]
    quarter = head_ref.shape[1]
    half = quarter // 2
    pre_rows = pre * n_kv
    tail = n_dp * pre_rows
    wide = -(-voc // 128) * 128
    step = wide // TILES
    tgt_ref[...] = jnp.zeros_like(tgt_ref)
    for kv, buf in enumerate(bufs):
        for pair in range(2):
            block = buf[:, pair * quarter : (pair + 1) * quarter].astype(F32)
            for j in range(2):
                row = (2 * pair + j) * pre_rows + pre * kv
                x_ref[row : row + pre, :] = block[pre * j : pre * (j + 1)]
        block = buf[:, 2 * quarter : 2 * quarter + half].astype(F32)
        for k in range(n_dp):
            row = tail + n_kv * k + kv
            x_ref[row : row + 1, :half] = block[k : k + 1]
            x_ref[row : row + 1, half:] = block[n_dp + k : n_dp + k + 1]
        digits = buf[:, 2 * quarter + half :].astype(F32)
        tgt_ref[pre * kv : pre * (kv + 1), :] = digits[:pre]
        tgt_ref[pre_rows + kv : pre_rows + kv + 1, :] = digits[pre : pre + 1]
    x = x_ref[...].astype(BF16)
    powers = []
    decs = []
    for t in range(TILES):
        start, stop = t * step, min((t + 1) * step, voc)
        y = lax.dot_general(
            x, head_ref[start:stop, :], (((1,), (1,)), ((), ())), preferred_element_type=F32
        )
        own_ref[:pre_rows, start:stop] = y[:pre_rows]
        own_ref[pre_rows : pre_rows + n_kv, start:stop] = y[tail : tail + n_kv]
        most = jnp.maximum(jnp.max(jnp.abs(y), axis=1, keepdims=True), TINY)
        power = jnp.ceil(jnp.log2(most * (1.0 / MOST)))
        powers.append(power)
        code = jnp.round(y * jnp.exp2(-power))
        if t == TILES - 1:
            last_ref[:, : stop - start] = code
            for i, p in enumerate(powers):
                last_ref[:, stop - start + i : stop - start + i + 1] = p
            code = last_ref[...]
        code = code.astype(jnp.int32)
        decs.append(code[tail:])
        for k in range(1, n_dp):
            for g in range(pre_rows // 8):
                low = k * pre_rows + 8 * g
                outs[k - 1][:, g * wide + start : g * wide + start + step] = code[low : low + 8].astype(WIRE)
    folds = 8 // n_kv
    for t in range(TILES // folds):
        for k in range(1, n_dp):
            both = [decs[t + f * (TILES // folds)][n_kv * k : n_kv * (k + 1)] for f in range(folds)]
            col = (pre_rows // 8) * wide + t * step
            outs[k - 1][:, col : col + step] = jnp.concatenate(both, axis=0).astype(WIRE)


def stats_kernel(pre, voc, chunks, *refs):
    out_ref, tile_ref = refs[-2:]
    tile_ref[...] = jnp.zeros_like(tile_ref)
    offset = lax.axis_index("vocab") * voc
    wide = -(-voc // 128) * 128
    step = wide // TILES
    spare = voc - (TILES - 1) * step
    for c in range(chunks):
        own_ref, *parts, tgt_ref = refs[5 * c : 5 * c + 5]
        n_kv = 8 // chunks
        pre_rows = pre * n_kv
        groups = pre_rows // 8

        def logits(piece, own):
            powers = [piece(p, TILES - 1)[:, spare : spare + TILES] for p in parts]
            tiles = []
            for t in range(TILES):
                stop = min(step, voc - t * step)
                total = own[:, t * step : t * step + stop]
                for p, power in zip(parts, powers):
                    total = total + piece(p, t)[:, :stop] * jnp.exp2(power[:, t : t + 1])
                tiles.append(total)
            return jnp.concatenate(tiles, axis=1)

        def pre_piece(g):
            return lambda p, t: p[:, g * wide + t * step : g * wide + (t + 1) * step].astype(F32)

        def dec_piece(p, t):
            per = TILES * n_kv // 8
            col = groups * wide + (t % per) * step
            low = n_kv * (t // per)
            return p[:, col : col + step].astype(F32)[low : low + n_kv]

        sets = [(8 * g, logits(pre_piece(g), own_ref[8 * g : 8 * g + 8, :])) for g in range(groups)]
        sets.append((pre_rows, logits(dec_piece, own_ref[pre_rows : pre_rows + n_kv, :])))
        s = jnp.concatenate([v for _, v in sets], axis=0)
        rows = s.shape[0]
        digits = tgt_ref[:rows]
        ids = digits[:, 0:1] + BASE * digits[:, 1:2] + (BASE * BASE) * digits[:, 2:3]
        local = ids.astype(jnp.int32) - offset
        columns = lax.broadcasted_iota(jnp.int32, s.shape, 1)
        top = jnp.max(s, axis=1, keepdims=True)
        total = jnp.sum(jnp.exp(s - top), axis=1, keepdims=True)
        picked = jnp.sum(jnp.where(columns == local, s, 0.0), axis=1, keepdims=True)
        lane = lax.broadcasted_iota(jnp.int32, (rows, 128), 1)
        st = jnp.where(lane == 0, top, jnp.where(lane == 1, total, picked))
        for kv in range(n_kv):
            at = BLOCK * (4 * (kv // (n_kv // 2)) + n_kv // 2 * c + kv % (n_kv // 2))
            tile_ref[at : at + pre, :] = st[pre * kv : pre * (kv + 1)]
            tile_ref[at + pre : at + pre + 1, :] = st[pre_rows + kv : pre_rows + kv + 1]
    out_ref[...] = jnp.transpose(tile_ref[...])[:8, :]


def merge(a, b):
    top = jnp.maximum(a[0:1], b[0:1])
    total = a[1:2] * jnp.exp(a[0:1] - top) + b[1:2] * jnp.exp(b[0:1] - top)
    return jnp.concatenate([top, total, a[2:3] + b[2:3]], axis=0)


def pair_kernel(mine_ref, other_ref, out_ref):
    other = pltpu.roll(other_ref[...], 64, 1)
    out_ref[0:3, :] = merge(mine_ref[...], other)
    out_ref[3:8, :] = jnp.zeros((5, 128), F32)


def final_kernel(pre, dec, mine_ref, r1, r2, r3, live_ref, pre_ref, dec_ref):
    total = mine_ref[...]
    for k, r in enumerate((r1, r2, r3), start=1):
        total = merge(total, pltpu.roll(r[...], 128 - BLOCK * k, 1))
    value = total[2:3] - (total[0:1] + jnp.log(total[1:2]))
    position = lax.axis_index("vocab") * dec
    pre_ref[...] = value[0, :pre]
    dec_ref[...] = jnp.where(position < live_ref[0, :dec], value[0, pre : pre + dec], 0.0)


def fast_body(n_dp, n_vocab, pre_hidden, dec_hidden, lm_head, pre_targets, dec_targets, dec_live):
    pre, dec = pre_hidden.shape[0], dec_hidden.shape[0]
    quarter, voc = lm_head.shape
    half = quarter // 2

    def swap(x, axis, k):
        return lax.ppermute(x, axis, [(i, i ^ k) for i in range(n_dp if axis == "dp" else n_vocab)])

    fold_width = half + -(-quarter // 1024) * 128
    pre_v, dec_v, *sends = call(
        load_kernel,
        [shape(pre_hidden.shape, BF16), shape(dec_hidden.shape, BF16)] + [shape((8, fold_width), BF16)] * (n_dp - 1),
        far(pre_hidden),
        far(dec_hidden),
        specs=[HBM] * 2,
        scratch=[pltpu.SemaphoreType.DMA((2,))],
    )
    ids, live = call(
        functools.partial(ids_kernel, pre),
        [shape((8, BASE), BF16), shape((1, 128), jnp.int32)],
        pre_targets,
        dec_targets,
        dec_live,
        specs=[SMEM] * 3,
    )
    wide = -(-voc // 128) * 128
    head = call(
        functools.partial(fetch_kernel, 8),
        shape((voc, quarter), BF16),
        far(lm_head.T),
        specs=[HBM],
        scratch=[pltpu.SemaphoreType.DMA((8,))],
        moved=4 * quarter * voc,
    )
    got = [swap(s, "dp", k) for k, s in enumerate(sends, start=1)]
    mine = call(dense_kernel, shape((8, 2 * quarter + half + BASE), BF16), pre_v, dec_v, *got, ids, specs=[VMEM] * 6)
    chips = [mine] + [swap(mine, "vocab", 2 * k) for k in (1, 2, 3)]
    cores = [swap(b, "vocab", 1) for b in chips]

    operands = []
    for c in range(CHUNKS):
        per = 4 // CHUNKS
        bufs = chips[per * c : per * (c + 1)] + cores[per * c : per * (c + 1)]
        group = len(bufs) * (pre + dec)
        rows = n_dp * group
        piece = shape((8, group * wide // 8), WIRE)
        own, *parts, tgt = call(
            functools.partial(matmul_kernel, n_dp, pre, voc),
            [shape((-(-group // 8) * 8, voc), F32)] + [piece] * (n_dp - 1) + [shape((-(-group // 8) * 8, BASE), F32)],
            head,
            *bufs,
            specs=[VMEM] * (1 + len(bufs)),
            scratch=[pltpu.VMEM((rows, quarter), F32), pltpu.VMEM((rows, wide // TILES), F32)],
            limit=16 << 20,
            flops=2 * rows * quarter * voc,
        )
        operands += [own] + [swap(p, "dp", k) for k, p in enumerate(parts, start=1)] + [tgt]
    stats = call(
        functools.partial(stats_kernel, pre, voc, CHUNKS),
        shape((8, 128), F32),
        *operands,
        specs=[VMEM] * len(operands),
        scratch=[pltpu.VMEM((128, 128), F32)],
    )
    both = call(pair_kernel, shape((8, 128), F32), stats, swap(stats, "vocab", 1), specs=[VMEM] * 2)
    others = [swap(both, "vocab", 2 * k) for k in (1, 2, 3)]
    return tuple(
        call(
            functools.partial(final_kernel, pre, dec),
            [shape((pre,), F32), shape((dec,), F32)],
            both,
            *others,
            live,
            specs=[VMEM] * 5,
        )
    )


def plain_body(pre_hidden, dec_hidden, lm_head, pre_targets, dec_targets, dec_live):
    pre, dec = pre_hidden.shape[0], dec_hidden.shape[0]
    own = pre + dec
    voc = lm_head.shape[1]
    hidden = jnp.concatenate([pre_hidden, dec_hidden], axis=0)
    targets = jnp.concatenate([pre_targets, dec_targets], axis=0)
    me = lax.axis_index("vocab")
    group_hidden = lax.all_gather(hidden, "vocab", axis=0, tiled=True)
    group_targets = lax.all_gather(targets, "vocab", axis=0, tiled=True)
    every = lax.all_to_all(group_hidden, "dp", split_axis=1, concat_axis=0, tiled=True)
    partial = jnp.dot(every, lm_head, preferred_element_type=F32)
    logits = lax.psum_scatter(partial, "dp", scatter_dimension=0, tiled=True)
    hit = (group_targets - me * voc)[:, None] == jnp.arange(voc, dtype=jnp.int32)[None, :]
    picked = jnp.sum(jnp.where(hit, logits, 0.0), axis=1)
    top = lax.pmax(jnp.max(logits, axis=1), "vocab")
    total = jnp.sum(jnp.exp(logits - top[:, None]), axis=1)
    total, picked = lax.psum((total, picked), "vocab")
    values = lax.dynamic_slice_in_dim(picked - (top + jnp.log(total)), me * own, own, 0)
    positions = me * dec + jnp.arange(dec, dtype=jnp.int32)
    return values[:pre], jnp.where(positions < dec_live[0], values[pre:], 0.0)


def solution(mesh):
    n_dp, n_vocab = mesh.shape["dp"], mesh.shape["vocab"]

    def body(pre_hidden, dec_hidden, lm_head, *rest):
        quarter, voc = lm_head.shape
        fits = (n_dp, n_vocab, pre_hidden.shape[0], dec_hidden.shape[0]) == (4, 8, 4, 1)
        fits = fits and quarter % 256 == 0 and TILES <= -voc % 128 and -(-voc // 128) % TILES == 0
        run = functools.partial(fast_body, n_dp, n_vocab) if fits else plain_body
        return run(pre_hidden, dec_hidden, lm_head, *rest)

    rows = P(("dp", "vocab"))
    in_specs = (P(("dp", "vocab"), None), P(("dp", "vocab"), None), P("dp", "vocab"), rows, rows, P("dp"))
    return jax.shard_map(body, mesh=mesh, in_specs=in_specs, out_specs=(rows, rows), check_vma=False)
```

```python
import functools

import jax
import jax.numpy as jnp
from jax import lax
from jax.experimental import pallas as pl
from jax.experimental.pallas import tpu as pltpu
from jax.sharding import PartitionSpec as P


BASE = 128
WIRE = jnp.int16
MOST = 32000.0
TINY = 1e-30
ROWS_CROSS = 1
TILES = 4
BLOCK = 16
VMEM = pl.BlockSpec(memory_space=pltpu.VMEM)
SMEM = pl.BlockSpec(memory_space=pltpu.SMEM)
HBM = pl.BlockSpec(memory_space=pltpu.HBM)
F32, BF16 = jnp.float32, jnp.bfloat16


def call(kernel, outs, *args, specs, scratch=(), limit=8 << 20, flops=0, moved=0):
    return pl.pallas_call(
        kernel,
        out_shape=outs,
        in_specs=specs,
        out_specs=jax.tree.map(lambda _: VMEM, outs),
        scratch_shapes=scratch,
        compiler_params=pltpu.CompilerParams(vmem_limit_bytes=limit),
        cost_estimate=pl.CostEstimate(flops=flops, bytes_accessed=moved, transcendentals=0),
    )(*args)


def far(x):
    return pltpu.with_memory_space_constraint(x, pltpu.HBM)


def shape(dims, dtype):
    return jax.ShapeDtypeStruct(dims, dtype)


def sublane(block):
    return lax.broadcasted_iota(jnp.int32, block, 0)


def spread(rows, block):
    out = jnp.zeros(block, F32)
    for i, row in rows.items():
        out = jnp.where(sublane(block) == i, jnp.broadcast_to(row, block), out)
    return out


def part(pre_ref, dec_ref, index):
    quarter = pre_ref.shape[1] // 4
    start = pl.multiple_of(index * quarter, 128)
    return pre_ref[:, pl.ds(start, quarter)].astype(F32), dec_ref[:, pl.ds(start, quarter)].astype(F32)


def near(other=False):
    core = lax.axis_index("vocab") & 1
    return 2 - core if other else 1 + core


def pack(pre, dec, out_ref, at):
    half = pre.shape[1] // 2
    width = half + dec_width(pre.shape[1])
    out_ref[:, at : at + half] = jnp.concatenate([pre[:, :half], pre[:, half:]], axis=0).astype(BF16)
    out_ref[:, at + half : at + width] = fold(dec).astype(BF16)


def unpack(block, quarter):
    half = quarter // 2
    pre = block[:, :half].astype(F32)
    return jnp.concatenate([pre[:4], pre[4:]], axis=1), unfold(block[:, half:].astype(F32), quarter)


def load_kernel(pre_hbm, dec_hbm, pt_hbm, pre_ref, dec_ref, cross_ref, diag_ref, ids_ref, pt_ref, sems):
    pairs = ((pre_hbm, pre_ref), (dec_hbm, dec_ref), (pt_hbm, pt_ref))
    copies = [pltpu.make_async_copy(src, dst, sems.at[i]) for i, (src, dst) in enumerate(pairs)]
    for c in copies:
        c.start()
    for c in copies:
        c.wait()
    me = lax.axis_index("dp")
    pack(*part(pre_ref, dec_ref, me ^ near(other=True)), cross_ref, 0)
    pack(*part(pre_ref, dec_ref, me ^ 3), diag_ref, 0)
    ids = jnp.zeros(ids_ref.shape, jnp.int32)
    for i in range(pre_ref.shape[0]):
        ids = jnp.where(sublane(ids.shape) == i, pt_ref[i], ids)
    ids_ref[...] = ids


def digits_kernel(pre, ids_ref, dt_ref, out_ref):
    ids = jnp.where(sublane(ids_ref.shape) == pre, dt_ref[0], ids_ref[...])
    lane = lax.broadcasted_iota(jnp.int32, ids.shape, 1)
    low, mid, high = ids & (BASE - 1), (ids >> 7) & (BASE - 1), ids >> 14
    out_ref[...] = jnp.where(lane == 0, low, jnp.where(lane == 1, mid, high)).astype(F32).astype(BF16)


def join_kernel(pre_ref, dec_ref, cross_ref, out_ref):
    pack(*part(pre_ref, dec_ref, lax.axis_index("dp") ^ near()), out_ref, 0)
    width = cross_ref.shape[1]
    out_ref[:, width:] = cross_ref[...]


def dec_width(quarter):
    return -(-quarter // 1024) * 128


def fold(row):
    each = -(-row.shape[1] // 1024) * 128
    rows = {}
    for i in range(8):
        low, high = min(i * each, row.shape[1]), min((i + 1) * each, row.shape[1])
        if high > low:
            rows[i] = row[:, low:high]
            if high - low < each:
                rows[i] = jnp.concatenate([rows[i], jnp.zeros((1, each - high + low), row.dtype)], axis=1)
    return spread(rows, (8, each))


def unfold(block, width):
    return jnp.concatenate([block[i : i + 1] for i in range(8)], axis=1)[:, :width]


def dense_kernel(pre_ref, dec_ref, near_ref, diag_ref, ids_ref, out_ref):
    sets = [part(pre_ref, dec_ref, lax.axis_index("dp"))]
    quarter = sets[0][0].shape[1]
    half = quarter // 2
    width = diag_ref.shape[1]
    for block in (near_ref[:, :width], near_ref[:, width:], diag_ref[...]):
        sets.append(unpack(block, quarter))
    for pair in range(2):
        both = jnp.concatenate([sets[2 * pair][0], sets[2 * pair + 1][0]], axis=0)
        out_ref[:, pair * quarter : (pair + 1) * quarter] = both.astype(BF16)
    rows = {k + 4 * h: s[1][:, h * half : (h + 1) * half] for k, s in enumerate(sets) for h in range(2)}
    out_ref[:, 2 * quarter : 2 * quarter + half] = spread(rows, (8, half)).astype(BF16)
    out_ref[:, 2 * quarter + half :] = ids_ref[...]


def fetch_kernel(parts, head_hbm, out_ref, sems):
    rows = out_ref.shape[0]
    step = -(-(rows // parts) // 8) * 8
    copies = []
    for i in range(parts):
        block = pl.ds(i * step, min((i + 1) * step, rows) - i * step)
        copies.append(pltpu.make_async_copy(head_hbm.at[block], out_ref.at[block], sems.at[i]))
    for c in copies:
        c.start()
    for c in copies:
        c.wait()


def tiles_of(voc):
    wide = -(-voc // 128) * 128
    step = wide // TILES
    return [(t * step, min((t + 1) * step, voc)) for t in range(TILES)]


def encode(tile, t, powers, out_ref, rows, last_ref):
    most = jnp.maximum(jnp.max(jnp.abs(tile), axis=1, keepdims=True), TINY)
    powers.append(jnp.ceil(jnp.log2(most * (1.0 / MOST))))
    code = jnp.round(tile * jnp.exp2(-powers[-1]))
    count, width = tile.shape
    step = out_ref[0].shape[1] // TILES
    if t == TILES - 1:
        last_ref[:count, :width] = code
        for i, p in enumerate(powers):
            last_ref[:count, width + i : width + i + 1] = p
        code = last_ref[:count]
    code = code.astype(jnp.int32)
    for i, ref in enumerate(out_ref):
        ref[:, t * step : (t + 1) * step] = code[i * rows : (i + 1) * rows].astype(WIRE)


def decode(ref, t, low, high, voc):
    power = ref[:, voc + t : voc + t + 1].astype(F32)
    return ref[:, low:high].astype(F32) * jnp.exp2(power)


def matmul_kernel(n_dp, pre, voc, origins, head_ref, *refs):
    n_kv = len(origins)
    bufs, refs = refs[:n_kv], refs[n_kv:]
    own_ref, outs, (tgt_ref, x_ref, last_ref) = refs[0], refs[1:n_dp], refs[n_dp:]
    quarter = head_ref.shape[1]
    half = quarter // 2
    pre_rows = pre * n_kv
    rows = pre_rows + n_kv
    for buf, (crossed, z) in zip(bufs, origins):
        blocks = [buf[:, i * quarter : (i + 1) * quarter].astype(F32) for i in range(2)]
        decs = buf[:, 2 * quarter : 2 * quarter + half].astype(F32)
        for place in range(n_dp):
            base = rows * (0, 1 + crossed, 1 + crossed, 3)[place]
            kv = n_kv // 2 * (crossed ^ (place % 2)) + z
            low = pre * (place % 2)
            x_ref[base + pre * kv : base + pre * (kv + 1), :] = blocks[place // 2][low : low + pre]
            row = base + pre_rows + kv
            x_ref[row : row + 1, :half] = decs[place : place + 1]
            x_ref[row : row + 1, half:] = decs[n_dp + place : n_dp + place + 1]
        kv = n_kv // 2 * crossed + z
        digits = buf[:, 2 * quarter + half :].astype(F32)
        tgt_ref[pre * kv : pre * (kv + 1), :] = digits[:pre]
        tgt_ref[pre_rows + kv : pre_rows + kv + 1, :] = digits[pre : pre + 1]
    x = x_ref[...].astype(BF16)
    powers = []
    for t, (low, high) in enumerate(tiles_of(voc)):
        y = lax.dot_general(x, head_ref[low:high, :], (((1,), (1,)), ((), ())), preferred_element_type=F32)
        own_ref[:, low:high] = y[:rows]
        encode(y[rows:], t, powers, outs, rows, last_ref)


def stats_kernel(pre, n_kv, own_ref, p1, p2, p3, tgt_ref, out_ref, tile_ref):
    tile_ref[...] = jnp.zeros_like(tile_ref)
    rows, voc = own_ref.shape
    pre_rows = pre * n_kv
    parts = []
    for t, (low, high) in enumerate(tiles_of(voc)):
        total = own_ref[:, low:high]
        for p in (p1, p2, p3):
            total = total + decode(p, t, low, high, voc)
        parts.append(total)
    s = jnp.concatenate(parts, axis=1)
    digits = tgt_ref[...]
    ids = digits[:, 0:1] + BASE * digits[:, 1:2] + (BASE * BASE) * digits[:, 2:3]
    local = ids.astype(jnp.int32) - lax.axis_index("vocab") * voc
    columns = lax.broadcasted_iota(jnp.int32, s.shape, 1)
    top = jnp.max(s, axis=1, keepdims=True)
    total = jnp.sum(jnp.exp(s - top), axis=1, keepdims=True)
    picked = jnp.sum(jnp.where(columns == local, s, 0.0), axis=1, keepdims=True)
    lane = lax.broadcasted_iota(jnp.int32, (rows, 128), 1)
    st = jnp.where(lane == 0, top, jnp.where(lane == 1, total, picked))
    for kv in range(n_kv):
        tile_ref[BLOCK * kv : BLOCK * kv + pre, :] = st[pre * kv : pre * (kv + 1)]
        tile_ref[BLOCK * kv + pre : BLOCK * kv + pre + 1, :] = st[pre_rows + kv : pre_rows + kv + 1]
    out_ref[...] = jnp.transpose(tile_ref[...])[:8, :]


def merge(a, b):
    top = jnp.maximum(a[0:1], b[0:1])
    total = a[1:2] * jnp.exp(a[0:1] - top) + b[1:2] * jnp.exp(b[0:1] - top)
    return jnp.concatenate([top, total, a[2:3] + b[2:3]], axis=0)


def pair_kernel(mine_ref, other_ref, out_ref):
    other = pltpu.roll(other_ref[...], 64, 1)
    out_ref[0:3, :] = merge(mine_ref[...], other)
    out_ref[3:8, :] = jnp.zeros((5, 128), F32)


def final_kernel(pre, dec, mine_ref, r1, r2, r3, live_ref, pre_ref, dec_ref):
    total = mine_ref[...]
    for k, r in enumerate((r1, r2, r3), start=1):
        total = merge(total, pltpu.roll(r[...], 64 - BLOCK * k, 1))
    value = total[2:3] - (total[0:1] + jnp.log(total[1:2]))
    position = lax.axis_index("vocab") * dec
    pre_ref[...] = value[0, :pre]
    dec_ref[...] = jnp.where(position < live_ref[0], value[0, pre : pre + dec], 0.0)


def fast_body(n_dp, n_vocab, pre_hidden, dec_hidden, lm_head, pre_targets, dec_targets, dec_live):
    pre, dec = pre_hidden.shape[0], dec_hidden.shape[0]
    quarter, voc = lm_head.shape
    half = quarter // 2

    def swap(x, steps):
        pairs = []
        for d in range(n_dp):
            for v in range(n_vocab):
                kd, kv = steps(v)
                pairs.append((d * n_vocab + v, (d ^ kd) * n_vocab + (v ^ kv)))
        return lax.ppermute(x, ("dp", "vocab"), pairs)

    def core(v):
        return 0, 1

    def near_chip(v):
        return 1 + v % 2, 1

    def far_chip(v):
        return 3, 1

    def along(k, crossing):
        return lambda v: (0, 2 * k + crossing)

    def near_a(v):
        return 2 - v % 2, 0

    def near_b(v):
        return 1 + v % 2, 0

    def diagonal(v):
        return 3, 0

    narrow = half + dec_width(quarter)
    wide = -(-voc // 128) * 128
    pre_v, dec_v, cross, diag, ids = call(
        load_kernel,
        [shape(pre_hidden.shape, BF16), shape(dec_hidden.shape, BF16)]
        + [shape((8, narrow), BF16)] * 2
        + [shape((8, BASE), jnp.int32)],
        *map(far, (pre_hidden, dec_hidden, pre_targets)),
        specs=[HBM] * 3,
        scratch=[pltpu.SMEM(pre_targets.shape, jnp.int32), pltpu.SemaphoreType.DMA((3,))],
    )
    ids = call(
        functools.partial(digits_kernel, pre), shape((8, BASE), BF16), ids, dec_targets, specs=[VMEM, SMEM]
    )
    cross = swap(cross, core)
    diag = swap(diag, far_chip)
    joined = call(join_kernel, shape((8, 2 * narrow), BF16), pre_v, dec_v, cross, specs=[VMEM] * 3)
    joined = swap(joined, near_chip)
    head = call(
        functools.partial(fetch_kernel, 8),
        shape((voc, quarter), BF16),
        far(lm_head.T),
        specs=[HBM],
        scratch=[pltpu.SemaphoreType.DMA((8,))],
        moved=4 * quarter * voc,
    )
    mine = call(
        dense_kernel,
        shape((8, 2 * quarter + half + BASE), BF16),
        pre_v,
        dec_v,
        joined,
        diag,
        ids,
        specs=[VMEM] * 5,
    )
    chips = [mine] + [swap(mine, along(k, ROWS_CROSS)) for k in (1, 2, 3)]
    bufs = chips + [swap(b, core) for b in chips]
    origins = [(0, 0)] + [(ROWS_CROSS, k) for k in (1, 2, 3)] + [(1, 0)] + [(1 - ROWS_CROSS, k) for k in (1, 2, 3)]
    group = n_vocab * (pre + dec)
    rows = n_dp * group
    own, *parts, tgt = call(
        functools.partial(matmul_kernel, n_dp, pre, voc, origins),
        [shape((group, voc), F32)] + [shape((group, wide), WIRE)] * (n_dp - 1) + [shape((group, BASE), F32)],
        head,
        *bufs,
        specs=[VMEM] * (1 + n_vocab),
        scratch=[pltpu.VMEM((rows, quarter), F32), pltpu.VMEM((rows - group, wide // TILES), F32)],
        limit=16 << 20,
        flops=2 * rows * quarter * voc,
    )
    parts = [swap(p, f) for p, f in zip(parts, (near_a, near_b, diagonal))]
    stats = call(
        functools.partial(stats_kernel, pre, n_vocab),
        shape((8, 128), F32),
        own,
        *parts,
        tgt,
        specs=[VMEM] * 5,
        scratch=[pltpu.VMEM((128, 128), F32)],
    )
    both = call(pair_kernel, shape((8, 128), F32), stats, swap(stats, core), specs=[VMEM] * 2)
    others = [swap(both, along(k, 1)) for k in (1, 2, 3)]
    return tuple(
        call(
            functools.partial(final_kernel, pre, dec),
            [shape((pre,), F32), shape((dec,), F32)],
            both,
            *others,
            dec_live,
            specs=[VMEM] * 4 + [SMEM],
        )
    )


def plain_body(pre_hidden, dec_hidden, lm_head, pre_targets, dec_targets, dec_live):
    pre, dec = pre_hidden.shape[0], dec_hidden.shape[0]
    own = pre + dec
    voc = lm_head.shape[1]
    hidden = jnp.concatenate([pre_hidden, dec_hidden], axis=0)
    targets = jnp.concatenate([pre_targets, dec_targets], axis=0)
    me = lax.axis_index("vocab")
    group_hidden = lax.all_gather(hidden, "vocab", axis=0, tiled=True)
    group_targets = lax.all_gather(targets, "vocab", axis=0, tiled=True)
    every = lax.all_to_all(group_hidden, "dp", split_axis=1, concat_axis=0, tiled=True)
    partial = jnp.dot(every, lm_head, preferred_element_type=F32)
    logits = lax.psum_scatter(partial, "dp", scatter_dimension=0, tiled=True)
    hit = (group_targets - me * voc)[:, None] == jnp.arange(voc, dtype=jnp.int32)[None, :]
    picked = jnp.sum(jnp.where(hit, logits, 0.0), axis=1)
    top = lax.pmax(jnp.max(logits, axis=1), "vocab")
    total = jnp.sum(jnp.exp(logits - top[:, None]), axis=1)
    total, picked = lax.psum((total, picked), "vocab")
    values = lax.dynamic_slice_in_dim(picked - (top + jnp.log(total)), me * own, own, 0)
    positions = me * dec + jnp.arange(dec, dtype=jnp.int32)
    return values[:pre], jnp.where(positions < dec_live[0], values[pre:], 0.0)


def solution(mesh):
    n_dp, n_vocab = mesh.shape["dp"], mesh.shape["vocab"]

    def body(pre_hidden, dec_hidden, lm_head, *rest):
        quarter, voc = lm_head.shape
        fits = (n_dp, n_vocab, pre_hidden.shape[0], dec_hidden.shape[0]) == (4, 8, 4, 1)
        fits = fits and quarter % 256 == 0 and TILES <= -voc % 128 and -(-voc // 128) % TILES == 0
        run = functools.partial(fast_body, n_dp, n_vocab) if fits else plain_body
        return run(pre_hidden, dec_hidden, lm_head, *rest)

    rows = P(("dp", "vocab"))
    in_specs = (P(("dp", "vocab"), None), P(("dp", "vocab"), None), P("dp", "vocab"), rows, rows, P("dp"))
    return jax.shard_map(body, mesh=mesh, in_specs=in_specs, out_specs=(rows, rows), check_vma=False)
```

```python
import functools

import jax
import jax.numpy as jnp
from jax import lax
from jax.experimental import pallas as pl
from jax.experimental.pallas import tpu as pltpu
from jax.sharding import PartitionSpec as P


BASE = 128
WIRE = jnp.int16
MOST = 32000.0
TINY = 1e-30
ROWS_CROSS = 1
TILES = 4
BLOCK = 16
VMEM = pl.BlockSpec(memory_space=pltpu.VMEM)
SMEM = pl.BlockSpec(memory_space=pltpu.SMEM)
HBM = pl.BlockSpec(memory_space=pltpu.HBM)
F32, BF16 = jnp.float32, jnp.bfloat16


def call(kernel, outs, *args, specs, out_specs=None, scratch=(), limit=8 << 20, flops=0, moved=0, aliases=None):
    return pl.pallas_call(
        kernel,
        out_shape=outs,
        in_specs=specs,
        out_specs=out_specs or jax.tree.map(lambda _: VMEM, outs),
        scratch_shapes=scratch,
        input_output_aliases=aliases or {},
        compiler_params=pltpu.CompilerParams(vmem_limit_bytes=limit),
        cost_estimate=pl.CostEstimate(flops=flops, bytes_accessed=moved, transcendentals=0),
    )(*args)


def far(x):
    return pltpu.with_memory_space_constraint(x, pltpu.HBM)


def shape(dims, dtype):
    return jax.ShapeDtypeStruct(dims, dtype)


def sublane(block):
    return lax.broadcasted_iota(jnp.int32, block, 0)


def spread(rows, block):
    out = jnp.zeros(block, F32)
    for i, row in rows.items():
        out = jnp.where(sublane(block) == i, jnp.broadcast_to(row, block), out)
    return out


def part(pre_ref, dec_ref, index):
    quarter = pre_ref.shape[1] // 4
    start = pl.multiple_of(index * quarter, 128)
    return pre_ref[:, pl.ds(start, quarter)].astype(F32), dec_ref[:, pl.ds(start, quarter)].astype(F32)


def near(other=False):
    core = lax.axis_index("vocab") & 1
    return 2 - core if other else 1 + core


def pack(pre, dec, out_ref, at):
    half = pre.shape[1] // 2
    width = half + dec_width(pre.shape[1])
    out_ref[:, at : at + half] = jnp.concatenate([pre[:, :half], pre[:, half:]], axis=0).astype(BF16)
    out_ref[:, at + half : at + width] = fold(dec).astype(BF16)


def unpack(block, quarter):
    half = quarter // 2
    pre = block[:, :half].astype(F32)
    return jnp.concatenate([pre[:4], pre[4:]], axis=1), unfold(block[:, half:].astype(F32), quarter)


def load_kernel(pre_hbm, dec_hbm, pt_hbm, pre_ref, dec_ref, cross_ref, diag_ref, ids_ref, pt_ref, sems):
    quarter = pre_ref.shape[1] // 4
    cuts = [pl.ds(i * quarter, quarter) for i in range(4)]
    pairs = [(pre_hbm.at[:, c], pre_ref.at[:, c]) for c in cuts] + [(dec_hbm, dec_ref), (pt_hbm, pt_ref)]
    copies = [pltpu.make_async_copy(src, dst, sems.at[i]) for i, (src, dst) in enumerate(pairs)]
    for c in copies:
        c.start()
    for c in copies:
        c.wait()
    me = lax.axis_index("dp")
    pack(*part(pre_ref, dec_ref, me ^ near(other=True)), cross_ref, 0)
    pack(*part(pre_ref, dec_ref, me ^ 3), diag_ref, 0)
    ids = jnp.zeros(ids_ref.shape, jnp.int32)
    for i in range(pre_ref.shape[0]):
        ids = jnp.where(sublane(ids.shape) == i, pt_ref[i], ids)
    ids_ref[...] = ids


def digits_kernel(pre, ids_ref, dt_ref, out_ref):
    ids = jnp.where(sublane(ids_ref.shape) == pre, dt_ref[0], ids_ref[...])
    lane = lax.broadcasted_iota(jnp.int32, ids.shape, 1)
    low, mid, high = ids & (BASE - 1), (ids >> 7) & (BASE - 1), ids >> 14
    out_ref[...] = jnp.where(lane == 0, low, jnp.where(lane == 1, mid, high)).astype(F32).astype(BF16)


def join_kernel(pre_ref, dec_ref, cross_ref, out_ref):
    pack(*part(pre_ref, dec_ref, lax.axis_index("dp") ^ near()), out_ref, 0)
    width = cross_ref.shape[1]
    out_ref[:, width:] = cross_ref[...]


def dec_width(quarter):
    return -(-quarter // 1024) * 128


def fold(row):
    each = -(-row.shape[1] // 1024) * 128
    rows = {}
    for i in range(8):
        low, high = min(i * each, row.shape[1]), min((i + 1) * each, row.shape[1])
        if high > low:
            rows[i] = row[:, low:high]
            if high - low < each:
                rows[i] = jnp.concatenate([rows[i], jnp.zeros((1, each - high + low), row.dtype)], axis=1)
    return spread(rows, (8, each))


def unfold(block, width):
    return jnp.concatenate([block[i : i + 1] for i in range(8)], axis=1)[:, :width]


def dense_kernel(pre_ref, dec_ref, near_ref, diag_ref, ids_ref, out_ref):
    sets = [part(pre_ref, dec_ref, lax.axis_index("dp"))]
    quarter = sets[0][0].shape[1]
    half = quarter // 2
    width = diag_ref.shape[1]
    for block in (near_ref[:, :width], near_ref[:, width:], diag_ref[...]):
        sets.append(unpack(block, quarter))
    for pair in range(2):
        both = jnp.concatenate([sets[2 * pair][0], sets[2 * pair + 1][0]], axis=0)
        out_ref[:, pair * quarter : (pair + 1) * quarter] = both.astype(BF16)
    rows = {k + 4 * h: s[1][:, h * half : (h + 1) * half] for k, s in enumerate(sets) for h in range(2)}
    out_ref[:, 2 * quarter : 2 * quarter + half] = spread(rows, (8, half)).astype(BF16)
    out_ref[:, 2 * quarter + half :] = ids_ref[...]


def fetch_kernel(parts, head_hbm, out_ref, sems):
    rows = out_ref.shape[0]
    step = -(-(rows // parts) // 8) * 8
    copies = []
    for i in range(parts):
        block = pl.ds(i * step, min((i + 1) * step, rows) - i * step)
        copies.append(pltpu.make_async_copy(head_hbm.at[block], out_ref.at[block], sems.at[i]))
    for c in copies:
        c.start()
    for c in copies:
        c.wait()


def tiles_of(voc):
    wide = -(-voc // 128) * 128
    step = wide // TILES
    return [(t * step, min((t + 1) * step, voc)) for t in range(TILES)]


def encode(tile, t, powers, out_ref, rows, last_ref):
    most = jnp.maximum(jnp.max(jnp.abs(tile), axis=1, keepdims=True), TINY)
    powers.append(jnp.ceil(jnp.log2(most * (1.0 / MOST))))
    code = jnp.round(tile * jnp.exp2(-powers[-1]))
    count, width = tile.shape
    step = out_ref[0].shape[1] // TILES
    if t == TILES - 1:
        last_ref[:count, :width] = code
        for i, p in enumerate(powers):
            last_ref[:count, width + i : width + i + 1] = p
        code = last_ref[:count]
    code = code.astype(jnp.int32)
    for i, ref in enumerate(out_ref):
        ref[:, t * step : (t + 1) * step] = code[i * rows : (i + 1) * rows].astype(WIRE)


def decode(ref, t, low, high, voc):
    power = ref[:, voc + t : voc + t + 1].astype(F32)
    return ref[:, low:high].astype(F32) * jnp.exp2(power)


def place_rows(n_kv, pre, bufs, origins, x_ref, tgt_ref):
    rows, quarter = x_ref.shape[0] // 4, x_ref.shape[1]
    half = quarter // 2
    pre_rows = pre * n_kv
    for buf, (crossed, z) in zip(bufs, origins):
        blocks = [buf[:, i * quarter : (i + 1) * quarter].astype(F32) for i in range(2)]
        decs = buf[:, 2 * quarter : 2 * quarter + half].astype(F32)
        for place in range(4):
            base = rows * (0, 1 + crossed, 1 + crossed, 3)[place]
            kv = n_kv // 2 * (crossed ^ (place % 2)) + z
            low = pre * (place % 2)
            x_ref[base + pre * kv : base + pre * (kv + 1), :] = blocks[place // 2][low : low + pre]
            row = base + pre_rows + kv
            x_ref[row : row + 1, :half] = decs[place : place + 1]
            x_ref[row : row + 1, half:] = decs[4 + place : 4 + place + 1]
        kv = n_kv // 2 * crossed + z
        digits = buf[:, 2 * quarter + half :].astype(F32)
        tgt_ref[pre * kv : pre * (kv + 1), :] = digits[:pre]
        tgt_ref[pre_rows + kv : pre_rows + kv + 1, :] = digits[pre : pre + 1]


def early_kernel(n_kv, pre, origins, *refs):
    place_rows(n_kv, pre, refs[:-2], origins, *refs[-2:])


def matmul_kernel(n_dp, n_kv, pre, voc, origins, head_ref, *refs):
    bufs, refs = refs[: len(origins)], refs[len(origins) + 2 :]
    own_ref, outs, (x_ref, tgt_ref, last_ref) = refs[0], refs[1:n_dp], refs[n_dp:]
    rows = x_ref.shape[0] // n_dp
    place_rows(n_kv, pre, bufs, origins, x_ref, tgt_ref)
    x = x_ref[...].astype(BF16)
    powers = []
    for t, (low, high) in enumerate(tiles_of(voc)):
        y = lax.dot_general(head_ref[low:high, :], x, (((1,), (1,)), ((), ())), preferred_element_type=F32)
        y = jnp.transpose(y)
        own_ref[:, low:high] = y[:rows]
        encode(y[rows:], t, powers, outs, rows, last_ref)


def stats_kernel(pre, n_kv, own_ref, p1, p2, p3, tgt_ref, out_ref, tile_ref):
    tile_ref[...] = jnp.zeros_like(tile_ref)
    rows, voc = own_ref.shape
    pre_rows = pre * n_kv
    parts = []
    for t, (low, high) in enumerate(tiles_of(voc)):
        total = own_ref[:, low:high]
        for p in (p1, p2, p3):
            total = total + decode(p, t, low, high, voc)
        parts.append(total)
    s = jnp.concatenate(parts, axis=1)
    digits = tgt_ref[...]
    ids = digits[:, 0:1] + BASE * digits[:, 1:2] + (BASE * BASE) * digits[:, 2:3]
    local = ids.astype(jnp.int32) - lax.axis_index("vocab") * voc
    columns = lax.broadcasted_iota(jnp.int32, s.shape, 1)
    top = jnp.max(s, axis=1, keepdims=True)
    total = jnp.sum(jnp.exp(s - top), axis=1, keepdims=True)
    picked = jnp.sum(jnp.where(columns == local, s, 0.0), axis=1, keepdims=True)
    lane = lax.broadcasted_iota(jnp.int32, (rows, 128), 1)
    st = jnp.where(lane == 0, top, jnp.where(lane == 1, total, picked))
    for kv in range(n_kv):
        tile_ref[BLOCK * kv : BLOCK * kv + pre, :] = st[pre * kv : pre * (kv + 1)]
        tile_ref[BLOCK * kv + pre : BLOCK * kv + pre + 1, :] = st[pre_rows + kv : pre_rows + kv + 1]
    out_ref[...] = jnp.transpose(tile_ref[...])[:8, :]


def merge(a, b):
    top = jnp.maximum(a[0:1], b[0:1])
    total = a[1:2] * jnp.exp(a[0:1] - top) + b[1:2] * jnp.exp(b[0:1] - top)
    return jnp.concatenate([top, total, a[2:3] + b[2:3]], axis=0)


def pair_kernel(mine_ref, other_ref, out_ref):
    other = pltpu.roll(other_ref[...], 64, 1)
    out_ref[0:3, :] = merge(mine_ref[...], other)
    out_ref[3:8, :] = jnp.zeros((5, 128), F32)


def final_kernel(pre, dec, mine_ref, r1, r2, r3, live_ref, pre_hbm, dec_hbm, pre_ref, dec_ref, sems):
    total = mine_ref[...]
    for k, r in enumerate((r1, r2, r3), start=1):
        total = merge(total, pltpu.roll(r[...], 64 - BLOCK * k, 1))
    value = total[2:3] - (total[0:1] + jnp.log(total[1:2]))
    position = lax.axis_index("vocab") * dec
    pre_ref[...] = value[0, :pre]
    dec_ref[...] = jnp.where(position < live_ref[0], value[0, pre : pre + dec], 0.0)
    copies = [
        pltpu.make_async_copy(pre_ref, pre_hbm, sems.at[0]),
        pltpu.make_async_copy(dec_ref, dec_hbm, sems.at[1]),
    ]
    for c in copies:
        c.start()
    for c in copies:
        c.wait()


def fast_body(n_dp, n_vocab, pre_hidden, dec_hidden, lm_head, pre_targets, dec_targets, dec_live):
    pre, dec = pre_hidden.shape[0], dec_hidden.shape[0]
    quarter, voc = lm_head.shape
    half = quarter // 2

    def swap(x, steps):
        pairs = []
        for d in range(n_dp):
            for v in range(n_vocab):
                kd, kv = steps(v)
                pairs.append((d * n_vocab + v, (d ^ kd) * n_vocab + (v ^ kv)))
        return lax.ppermute(x, ("dp", "vocab"), pairs)

    def core(v):
        return 0, 1

    def near_chip(v):
        return 1 + v % 2, 1

    def far_chip(v):
        return 3, 1

    def along(k, crossing):
        return lambda v: (0, 2 * k + crossing)

    def near_a(v):
        return 2 - v % 2, 0

    def near_b(v):
        return 1 + v % 2, 0

    def diagonal(v):
        return 3, 0

    narrow = half + dec_width(quarter)
    wide = -(-voc // 128) * 128
    pre_v, dec_v, cross, diag, ids = call(
        load_kernel,
        [shape(pre_hidden.shape, BF16), shape(dec_hidden.shape, BF16)]
        + [shape((8, narrow), BF16)] * 2
        + [shape((8, BASE), jnp.int32)],
        *map(far, (pre_hidden, dec_hidden, pre_targets)),
        specs=[HBM] * 3,
        scratch=[pltpu.SMEM(pre_targets.shape, jnp.int32), pltpu.SemaphoreType.DMA((6,))],
    )
    ids = call(
        functools.partial(digits_kernel, pre), shape((8, BASE), BF16), ids, dec_targets, specs=[VMEM, SMEM]
    )
    cross = swap(cross, core)
    diag = swap(diag, far_chip)
    joined = call(join_kernel, shape((8, 2 * narrow), BF16), pre_v, dec_v, cross, specs=[VMEM] * 3)
    joined = swap(joined, near_chip)
    head = call(
        functools.partial(fetch_kernel, 8),
        shape((voc, quarter), BF16),
        far(lm_head.T),
        specs=[HBM],
        scratch=[pltpu.SemaphoreType.DMA((8,))],
        moved=4 * quarter * voc,
    )
    mine = call(
        dense_kernel,
        shape((8, 2 * quarter + half + BASE), BF16),
        pre_v,
        dec_v,
        joined,
        diag,
        ids,
        specs=[VMEM] * 5,
    )
    chips = [mine] + [swap(mine, along(k, ROWS_CROSS)) for k in (1, 2, 3)]
    bufs = chips + [swap(b, core) for b in chips]
    origins = [(0, 0)] + [(ROWS_CROSS, k) for k in (1, 2, 3)] + [(1, 0)] + [(1 - ROWS_CROSS, k) for k in (1, 2, 3)]
    group = n_vocab * (pre + dec)
    rows = n_dp * group
    late = 1
    placed = [shape((rows, quarter), F32), shape((group, BASE), F32)]
    placed_rows = call(
        functools.partial(early_kernel, n_vocab, pre, origins[:-late]),
        placed,
        *bufs[:-late],
        specs=[VMEM] * (len(bufs) - late),
    )
    own, *parts, _, tgt = call(
        functools.partial(matmul_kernel, n_dp, n_vocab, pre, voc, origins[-late:]),
        [shape((group, voc), F32)] + [shape((group, wide), WIRE)] * (n_dp - 1) + placed,
        head,
        *bufs[-late:],
        *placed_rows,
        specs=[VMEM] * (3 + late),
        scratch=[pltpu.VMEM((rows - group, wide // TILES), F32)],
        limit=16 << 20,
        flops=2 * rows * quarter * voc,
        aliases={1 + late: n_dp, 2 + late: n_dp + 1},
    )
    parts = [swap(p, f) for p, f in zip(parts, (near_a, near_b, diagonal))]
    stats = call(
        functools.partial(stats_kernel, pre, n_vocab),
        shape((8, 128), F32),
        own,
        *parts,
        tgt,
        specs=[VMEM] * 5,
        scratch=[pltpu.VMEM((128, 128), F32)],
    )
    both = call(pair_kernel, shape((8, 128), F32), stats, swap(stats, core), specs=[VMEM] * 2)
    others = [swap(both, along(k, 1)) for k in (1, 2, 3)]
    return tuple(
        call(
            functools.partial(final_kernel, pre, dec),
            [shape((pre,), F32), shape((dec,), F32)],
            both,
            *others,
            dec_live,
            specs=[VMEM] * 4 + [SMEM],
            out_specs=[HBM] * 2,
            scratch=[pltpu.VMEM((pre,), F32), pltpu.VMEM((dec,), F32), pltpu.SemaphoreType.DMA((2,))],
        )
    )


def plain_body(pre_hidden, dec_hidden, lm_head, pre_targets, dec_targets, dec_live):
    pre, dec = pre_hidden.shape[0], dec_hidden.shape[0]
    own = pre + dec
    voc = lm_head.shape[1]
    hidden = jnp.concatenate([pre_hidden, dec_hidden], axis=0)
    targets = jnp.concatenate([pre_targets, dec_targets], axis=0)
    me = lax.axis_index("vocab")
    group_hidden = lax.all_gather(hidden, "vocab", axis=0, tiled=True)
    group_targets = lax.all_gather(targets, "vocab", axis=0, tiled=True)
    every = lax.all_to_all(group_hidden, "dp", split_axis=1, concat_axis=0, tiled=True)
    partial = jnp.dot(every, lm_head, preferred_element_type=F32)
    logits = lax.psum_scatter(partial, "dp", scatter_dimension=0, tiled=True)
    hit = (group_targets - me * voc)[:, None] == jnp.arange(voc, dtype=jnp.int32)[None, :]
    picked = jnp.sum(jnp.where(hit, logits, 0.0), axis=1)
    top = lax.pmax(jnp.max(logits, axis=1), "vocab")
    total = jnp.sum(jnp.exp(logits - top[:, None]), axis=1)
    total, picked = lax.psum((total, picked), "vocab")
    values = lax.dynamic_slice_in_dim(picked - (top + jnp.log(total)), me * own, own, 0)
    positions = me * dec + jnp.arange(dec, dtype=jnp.int32)
    return values[:pre], jnp.where(positions < dec_live[0], values[pre:], 0.0)


def solution(mesh):
    n_dp, n_vocab = mesh.shape["dp"], mesh.shape["vocab"]

    def body(pre_hidden, dec_hidden, lm_head, *rest):
        quarter, voc = lm_head.shape
        fits = (n_dp, n_vocab, pre_hidden.shape[0], dec_hidden.shape[0]) == (4, 8, 4, 1)
        fits = fits and quarter % 256 == 0 and TILES <= -voc % 128 and -(-voc // 128) % TILES == 0
        run = functools.partial(fast_body, n_dp, n_vocab) if fits else plain_body
        return run(pre_hidden, dec_hidden, lm_head, *rest)

    rows = P(("dp", "vocab"))
    in_specs = (P(("dp", "vocab"), None), P(("dp", "vocab"), None), P("dp", "vocab"), rows, rows, P("dp"))
    return jax.shard_map(body, mesh=mesh, in_specs=in_specs, out_specs=(rows, rows), check_vma=False)
```
